32 devices in a mesh: vox: 8 (over z, y), frm: 4 (over x, core).
Axes of the slice: x: 2, y: 2, z: 4, core: 2. Of those that a mesh axis runs over, the one named last changes fastest.
Arguments:
- data: bfloat16 [32768, 1024], P('vox', 'frm'), may hold values from -6 to 10.375
- footprints: bfloat16 [64, 4, 512, 128], P('vox'), may hold values from 0 to 1, as said below
- traces: bfloat16 [64, 128, 1024], P('vox', None, 'frm'), may hold values from 0 to 1
- incidence: int32 [64, 4], replicated, may hold values from 0 to 63, as said below
- counts: int32 [64], replicated, may hold values from 1 to 128
Outputs:
- new_traces: bfloat16 [64, 128, 1024], P('vox', None, 'frm')
- new_footprints: bfloat16 [64, 4, 512, 128], P('vox', None, 'frm')
The draws below stay inside these ranges and needn't reach their ends.
Inputs may be any that keep to these rules, and one draw needn't show every extreme that they name: `incidence`: neuron block j is owned by the device of vox index j // 8. Among the 32 entries of one device's voxel blocks, at most 8 name blocks of one owner, and exactly 8 do for some owner. Over all devices, the blocks of each owner are named exactly 8 * 4 times, and every neuron block is named at least once. `footprints`: every entry is 0 or positive; every neuron column of every tile has a positive entry.
All inputs are finite; a program needn't handle non-finite values.
Results may differ from the reference program's by a relative error of at most 0.0034.
Values may be sent and summed in bfloat16 or wider, within the bound.
A program may use at most 128 MiB of HBM per device.

```python
import math
import jax
import jax.numpy as jnp
from jax import lax

BV = 512
BN = 128
K = 4
VB_DEV = 8
NB_DEV = 8
VBLOCKS = 64
NBLOCKS = 64
VOXELS = 32768
FRAMES = 1024
CAP = 8
N_VOX = 8


def draw_footprints(key, part):
    key_value, key_spread, key_pinned = jax.random.split(key, 3)
    shape = (VBLOCKS, K, BV, BN)
    values = jnp.exp(jax.random.uniform(key_value, shape, jnp.float32, math.log(0.25), 0.0))
    spread = jax.random.uniform(key_spread, shape, jnp.float32) < 1.0 / 32.0
    pinned = jax.random.randint(key_pinned, (VBLOCKS, K, 1, BN), 0, BV)
    voxel_rows = jnp.arange(BV, dtype=jnp.int32)[None, None, :, None]
    return jnp.where(spread | (voxel_rows == pinned), values, 0.0).astype(jnp.bfloat16)


def draw_incidence(key, part):
    key_first, key_pool, key_shift, key_order = jax.random.split(key, 4)
    entries = VB_DEV * K
    pool_size = N_VOX * CAP
    position = jnp.arange(pool_size, dtype=jnp.int32)
    pool = position % N_VOX
    first = jax.random.randint(key_first, (), 0, N_VOX)
    shuffled = jax.random.permutation(key_pool, pool_size).astype(jnp.int32)
    wanted = (pool == 1) | (pool == N_VOX - 1) | (pool == N_VOX // 2)
    forced = wanted & (position < N_VOX) & (pool != first)
    scores = jnp.where(pool == first, position, jnp.where(forced, pool_size + position, 2 * pool_size + shuffled))
    ranking = jnp.argsort(scores)
    offsets = pool[ranking[:entries]]
    shifts = jax.random.randint(key_shift, (N_VOX,), 0, NB_DEV)
    source = jnp.arange(N_VOX, dtype=jnp.int32)[:, None]
    owners = (source + offsets[None, :]) % N_VOX
    entry_index = jnp.arange(entries, dtype=jnp.int32)[None, :]
    within = (entry_index + shifts[owners]) % NB_DEV
    named = owners * NB_DEV + within
    row_keys = jax.random.split(key_order, N_VOX)

    def shuffle_row(subkey):
        return jax.random.permutation(subkey, entries)
    orders = jax.vmap(shuffle_row)(row_keys).astype(jnp.int32)
    placed = jnp.take_along_axis(named, orders, axis=1)
    return placed.reshape(VBLOCKS, K).astype(jnp.int32)


def set_ends(drawn, own_key, smallest, largest):
    longest = drawn.shape.index(max(drawn.shape))
    spots = []
    for shift in (0, 1):
        where = [jax.random.randint(jax.random.fold_in(own_key, axis), (), 0, length) for axis, length in enumerate(drawn.shape)]
        where[longest] = (where[longest] + shift) % drawn.shape[longest]
        spots.append(tuple(where))
    return drawn.at[spots[0]].set(smallest).at[spots[1]].set(largest)


def shard_levels(stream_key, shape, cuts, smallest, largest):
    def one(dim, shards_of):
        heights = jax.random.uniform(jax.random.fold_in(jax.random.fold_in(stream_key, 6), dim), (shards_of,), jnp.float32, smallest / len(cuts), largest / len(cuts))
        return jnp.repeat(jnp.exp(heights), shape[dim] // shards_of).reshape((-1,) + (1,) * (len(shape) - dim - 1))

    loudness = one(*cuts[0])
    for cut in cuts[1:]:
        loudness = loudness * one(*cut)
    return loudness


def setup_inputs(seed: int = 0) -> dict:
    seeds = jax.random.split(jax.random.key(seed), 6)
    return {
        "data": jnp.clip(-6.0 + 16.375 * jax.random.uniform(seeds[0], (VOXELS, FRAMES), jnp.float32) ** shard_levels(seeds[0], (VOXELS, FRAMES), ((0, 8), (1, 4)), -0.2, 0.2), -6.0, 10.375).astype(jnp.bfloat16),
        "footprints": draw_footprints(jax.random.fold_in(seeds[5], 71), 0),
        "traces": jnp.clip(1.0 * jax.random.uniform(seeds[2], (NBLOCKS, BN, FRAMES), jnp.float32) ** shard_levels(seeds[2], (NBLOCKS, BN, FRAMES), ((0, 8), (2, 4)), -0.2, 0.2), 0.0, 1.0).astype(jnp.bfloat16),
        "incidence": draw_incidence(jax.random.fold_in(seeds[5], 71), 0),
        "counts": set_ends(jax.random.randint(seeds[4], (NBLOCKS,), 1, BN + 1), jax.random.fold_in(seeds[4], 1), 1, BN).astype(jnp.int32),
    }


highest = lax.Precision.HIGHEST


def reference(data, footprints, traces, incidence, counts):
    neuron = jnp.arange(BN, dtype=jnp.int32)
    live = neuron[None, :] < counts[:, None]
    alive = jnp.where(live[:, :, None], traces, jnp.zeros((), traces.dtype))
    blocks = data.reshape(VBLOCKS, BV, FRAMES)

    def residual(vblock, source):
        picked = source[incidence[vblock]]
        recon = jnp.einsum('kxn,knf->xf', footprints[vblock].astype(jnp.float32), picked.astype(jnp.float32), precision=highest)
        resid = (blocks[vblock].astype(jnp.float32) - recon).astype(jnp.bfloat16)
        return resid, picked

    def trace_step(carry, vblock):
        grad, denom = carry
        resid, unused = residual(vblock, alive)
        tiles = footprints[vblock].astype(jnp.float32)
        term = jnp.einsum('kxn,xf->knf', tiles, resid.astype(jnp.float32), precision=highest)
        rowsum = jnp.sum(tiles, axis=(0, 2))
        dterm = jnp.einsum('kxn,x->kn', tiles, rowsum, precision=highest)
        named = incidence[vblock]
        return (grad.at[named].add(term), denom.at[named].add(dterm)), None

    start = (jnp.zeros((NBLOCKS, BN, FRAMES), jnp.float32), jnp.zeros((NBLOCKS, BN), jnp.float32))
    (grad, denom), unused = lax.scan(trace_step, start, jnp.arange(VBLOCKS, dtype=jnp.int32))
    updated = jnp.maximum(traces.astype(jnp.float32) + grad / denom[:, :, None], 0.0)
    new_traces = jnp.where(live[:, :, None], updated, 0.0).astype(jnp.bfloat16)

    def foot_step(vblock):
        resid, picked = residual(vblock, new_traces)
        fgrad = jnp.einsum('xf,knf->kxn', resid.astype(jnp.float32), picked.astype(jnp.float32), precision=highest)
        power = jnp.sum(jnp.square(picked.astype(jnp.float32)), axis=2)
        tiles = footprints[vblock]
        keep = live[incidence[vblock]][:, None, :] & (tiles > 0)
        moved = jnp.maximum(tiles.astype(jnp.float32) + fgrad / jnp.maximum(power, 1.0)[:, None, :], 0.0)
        return jnp.where(keep, moved, 0.0).astype(jnp.bfloat16)

    new_footprints = lax.map(foot_step, jnp.arange(VBLOCKS, dtype=jnp.int32))
    return new_traces, new_footprints
```

```python
import functools
import jax
import jax.numpy as jnp
from jax import lax
from jax.experimental import pallas as pl
from jax.experimental.pallas import tpu as pltpu
from jax.sharding import PartitionSpec as P

VMEM = pltpu.VMEM
NT = (((1,), (1,)), ((), ()))
TN = (((0,), (0,)), ((), ()))


def matmul(a, b, dims=(((1,), (0,)), ((), ()))):
    return lax.dot_general(a, b, dims, preferred_element_type=jnp.float32)


def split_two(value):
    high = value.astype(jnp.bfloat16)
    return high, (value - high.astype(jnp.float32)).astype(jnp.bfloat16)


def ring_position(index, n):
    odd = lax.rem(index, 2)
    half = index // 2
    return (1 - odd) * half + odd * (n - 1 - half)


def ring_index(position, n):
    q = lax.rem(position + 2 * n, n)
    upper = q // (n // 2)
    return (1 - upper) * 2 * q + upper * (2 * n - 1 - 2 * q)


def greet(peers):
    barrier = pltpu.get_barrier_semaphore()
    for peer in peers:
        pl.semaphore_signal(
            barrier, inc=1, device_id=peer, device_id_type=pl.DeviceIdType.MESH
        )
    pl.semaphore_wait(barrier, len(peers))


class Ring:
    def __init__(self, n, nb, subs):
        self.n, self.nb, self.subs = n, nb, subs
        self.hops = n // 2
        self.step = nb // subs
        self.me = lax.axis_index("vox")
        self.pos = ring_position(self.me, n)
        self.next = (ring_index(self.pos + 1, n), ring_index(self.pos - 1, n))

    def owner(self, way, distance):
        return ring_index(self.pos + (distance if way == 0 else -distance), self.n)

    def rows(self, owner, sub):
        return pl.ds(owner * self.nb + sub * self.step, self.step)

    def far_part(self, way, sub):
        return (sub < self.subs // 2) == (way == 0)

    def copy(self, src, dst, send, recv, way):
        return pltpu.make_async_remote_copy(
            src_ref=src,
            dst_ref=dst,
            send_sem=send,
            recv_sem=recv,
            device_id={"vox": self.next[way]},
            device_id_type=pl.DeviceIdType.MESH,
        )


def gather_copy(ring, own, full, send, recv, way, hop, sub):
    rows = ring.rows(ring.owner(way, -hop), sub)
    src = own.at[pl.ds(sub * ring.step, ring.step)] if hop == 0 else full.at[rows]
    return ring.copy(src, full.at[rows], send.at[way, hop, sub], recv.at[way, hop, sub], way)


def gather_rest(ring, own, full, send, recv):
    copy = functools.partial(gather_copy, ring, own, full, send, recv)
    last = ring.hops - 1

    def used(way, hop, sub):
        return hop < last or ring.far_part(way, sub)

    for hop in range(1, ring.hops + 1):
        for sub in range(ring.subs):
            for way in range(2):
                if used(way, hop - 1, sub):
                    copy(way, hop - 1, sub).wait_recv()
                    if hop <= last and used(way, hop, sub):
                        copy(way, hop, sub).start()
    for hop in range(ring.hops):
        for sub in range(ring.subs):
            for way in range(2):
                if used(way, hop, sub):
                    copy(way, hop, sub).wait_send()


def gather_kernel(n, subs, own, full, send, recv):
    nb = own.shape[0]
    ring = Ring(n, nb, subs)
    greet([{"vox": peer} for peer in ring.next])
    for sub in range(subs):
        for way in range(2):
            gather_copy(ring, own, full, send, recv, way, 0, sub).start()
    full[pl.ds(ring.me * nb, nb)] = own[...]
    gather_rest(ring, own, full, send, recv)


def gather_traces(traces, n, subs):
    nb, bn, t = traces.shape
    return pl.pallas_call(
        functools.partial(gather_kernel, n, subs),
        out_shape=jax.ShapeDtypeStruct((n * nb, bn, t), jnp.bfloat16),
        in_specs=[pl.BlockSpec(memory_space=VMEM)],
        out_specs=pl.BlockSpec(memory_space=VMEM),
        scratch_shapes=[
            pltpu.SemaphoreType.DMA((2, n // 2, subs)),
            pltpu.SemaphoreType.DMA((2, n // 2, subs)),
        ],
        compiler_params=pltpu.CompilerParams(collective_id=0, has_side_effects=True),
        name="gather_traces",
    )(traces)


def recon_of(foot, entries):
    total = None
    for tile, entry in zip(foot, entries):
        part = matmul(tile, entry)
        total = part if total is None else total + part
    return total


def term_kernel(block_ref, counts_ref, foot_ref, data_ref, full_ref, part_ref, denom_ref, total):
    step = pl.program_id(0)
    touches, _, bn = foot_ref.shape[1:]

    @pl.when(step == 0)
    def _():
        total[...] = jnp.zeros_like(total)
        denom_ref[...] = jnp.zeros_like(denom_ref)

    foot = [foot_ref[0, k] for k in range(touches)]
    named = [block_ref[step, k] for k in range(touches)]
    neuron = lax.broadcasted_iota(jnp.int32, full_ref.shape[1:], 0)
    entries = [
        jnp.where(neuron < counts_ref[j], full_ref[j], jnp.zeros((), jnp.bfloat16)) for j in named
    ]
    resid = (data_ref[...].astype(jnp.float32) - recon_of(foot, entries)).astype(jnp.bfloat16)
    ones = jnp.ones((8, bn), jnp.bfloat16)
    rowsum = None
    for tile in foot:
        part = matmul(ones, tile, NT)
        rowsum = part if rowsum is None else rowsum + part
    high, low = split_two(rowsum)
    for k, j in enumerate(named):
        total[j] += matmul(foot[k], resid, TN)
        dterm = matmul(high, foot[k]) + matmul(low, foot[k])
        denom_ref[pl.ds(j, 1), :] += dterm[:1]

    @pl.when(step == pl.num_programs(0) - 1)
    def _():
        part_ref[...] = total[...].astype(jnp.bfloat16)


def terms(my_block, counts, footprints, data, full):
    vblocks, touches, bv, bn = footprints.shape
    blocks, _, t = full.shape
    return pl.pallas_call(
        term_kernel,
        out_shape=(
            jax.ShapeDtypeStruct(full.shape, jnp.bfloat16),
            jax.ShapeDtypeStruct((blocks, bn), jnp.float32),
        ),
        grid_spec=pltpu.PrefetchScalarGridSpec(
            num_scalar_prefetch=2,
            grid=(vblocks,),
            in_specs=[
                pl.BlockSpec((1, touches, bv, bn), lambda i, *_: (i, 0, 0, 0)),
                pl.BlockSpec((bv, t), lambda i, *_: (i, 0)),
                pl.BlockSpec((blocks, bn, t), lambda i, *_: (0, 0, 0)),
            ],
            out_specs=(
                pl.BlockSpec((blocks, bn, t), lambda i, *_: (0, 0, 0)),
                pl.BlockSpec((blocks, bn), lambda i, *_: (0, 0)),
            ),
            scratch_shapes=[pltpu.VMEM((blocks, bn, t), jnp.float32)],
        ),
        name="terms",
    )(my_block, counts, footprints, data, full)


def update_kernel(
    n, subs, part, denom, own, live, new, full, got, out, dgot, send, recv, dsend, drecv, asend, arecv
):
    nb = own.shape[0]
    ring = Ring(n, nb, subs)
    hops = ring.hops
    peers = [lax.rem(ring.me + k, n) for k in range(1, n)]
    greet([{"vox": peer} for peer in peers])

    def used(way, hop, sub):
        return hop > 0 or ring.far_part(way, sub)

    def piece(sub):
        return pl.ds(sub * ring.step, ring.step)

    def copy(way, hop, sub):
        rows = ring.rows(ring.owner(way, hops - hop), sub)
        first = hop == 0 or not used(way, hop - 1, sub)
        src = part.at[rows] if first else out.at[way, hop, piece(sub)]
        return ring.copy(
            src, got.at[way, hop, piece(sub)], send.at[way, hop, sub], recv.at[way, hop, sub], way
        )

    def dcopy(k):
        peer = peers[k - 1]
        return pltpu.make_async_remote_copy(
            src_ref=denom.at[peer],
            dst_ref=dgot.at[k - 1],
            send_sem=dsend.at[k - 1],
            recv_sem=drecv.at[k - 1],
            device_id={"vox": peer},
            device_id_type=pl.DeviceIdType.MESH,
        )

    for hop in range(hops):
        for sub in range(subs):
            for way in range(2):
                if not used(way, hop, sub):
                    continue
                if hop > 0 and used(way, hop - 1, sub):
                    copy(way, hop - 1, sub).wait_recv()
                    rows = ring.rows(ring.owner(way, hops - hop), sub)
                    summed = got[way, hop - 1, piece(sub)].astype(jnp.float32) + part[rows].astype(
                        jnp.float32
                    )
                    out[way, hop, piece(sub)] = summed.astype(jnp.bfloat16)
                copy(way, hop, sub).start()
        if hop == 0:
            for k in range(1, n):
                dcopy(k).start()
    total = denom[ring.me]
    for k in range(1, n):
        dcopy(k).wait_recv()
        total = total + dgot[k - 1]
    columns = jnp.transpose(total)
    alive = jnp.transpose(live[...])
    for sub in range(subs):
        for way in range(2):
            copy(way, hops - 1, sub).wait_recv()
        rows = ring.rows(ring.me, sub)
        grad = part[rows].astype(jnp.float32)
        for way in range(2):
            grad = grad + got[way, hops - 1, piece(sub)].astype(jnp.float32)
        for b in range(ring.step):
            j = sub * ring.step + b
            moved = own[j].astype(jnp.float32) + grad[b] / columns[:, j : j + 1]
            moved = jnp.where(alive[:, j : j + 1] > 0, jnp.maximum(moved, 0.0), 0.0)
            new[j] = moved.astype(jnp.bfloat16)
        for way in range(2):
            gather_copy(ring, new, full, asend, arecv, way, 0, sub).start()
    full[pl.ds(ring.me * nb, nb)] = new[...]
    gather_rest(ring, new, full, asend, arecv)
    for hop in range(hops):
        for sub in range(subs):
            for way in range(2):
                if used(way, hop, sub):
                    copy(way, hop, sub).wait_send()
    for k in range(1, n):
        dcopy(k).wait_send()


def update_traces(part, denom, traces, live, n, subs):
    nb, bn, t = traces.shape
    hops = n // 2
    return pl.pallas_call(
        functools.partial(update_kernel, n, subs),
        out_shape=(
            jax.ShapeDtypeStruct(traces.shape, jnp.bfloat16),
            jax.ShapeDtypeStruct(part.shape, jnp.bfloat16),
        ),
        in_specs=[pl.BlockSpec(memory_space=VMEM)] * 4,
        out_specs=(pl.BlockSpec(memory_space=VMEM),) * 2,
        scratch_shapes=[
            pltpu.VMEM((2, hops, nb, bn, t), jnp.bfloat16),
            pltpu.VMEM((2, hops, nb, bn, t), jnp.bfloat16),
            pltpu.VMEM((n - 1, nb, bn), jnp.float32),
            pltpu.SemaphoreType.DMA((2, hops, subs)),
            pltpu.SemaphoreType.DMA((2, hops, subs)),
            pltpu.SemaphoreType.DMA((n - 1,)),
            pltpu.SemaphoreType.DMA((n - 1,)),
            pltpu.SemaphoreType.DMA((2, hops, subs)),
            pltpu.SemaphoreType.DMA((2, hops, subs)),
        ],
        compiler_params=pltpu.CompilerParams(collective_id=1, has_side_effects=True),
        name="update_traces",
    )(part, denom.reshape(n, nb, bn), traces, live)


def foot_kernel(block_ref, foot_ref, data_ref, full_ref, grad_ref, power_ref):
    step = pl.program_id(0)
    touches, _, bn = foot_ref.shape[1:]
    foot = [foot_ref[0, k] for k in range(touches)]
    entries = [full_ref[block_ref[step, k]] for k in range(touches)]
    resid = (data_ref[...].astype(jnp.float32) - recon_of(foot, entries)).astype(jnp.bfloat16)
    ones = jnp.ones((8, full_ref.shape[2]), jnp.bfloat16)
    for k, entry in enumerate(entries):
        grad_ref[0, k] = matmul(resid, entry, NT).astype(jnp.bfloat16)
        wide = entry.astype(jnp.float32)
        high, low = split_two(wide * wide)
        squares = matmul(ones, high, NT) + matmul(ones, low, NT)
        power_ref[0, k : k + 1, :] = squares[:1]


def foot_terms(my_block, footprints, data, full):
    vblocks, touches, bv, bn = footprints.shape
    blocks, _, t = full.shape
    return pl.pallas_call(
        foot_kernel,
        out_shape=(
            jax.ShapeDtypeStruct(footprints.shape, jnp.bfloat16),
            jax.ShapeDtypeStruct((vblocks, touches, bn), jnp.float32),
        ),
        grid_spec=pltpu.PrefetchScalarGridSpec(
            num_scalar_prefetch=1,
            grid=(vblocks,),
            in_specs=[
                pl.BlockSpec((1, touches, bv, bn), lambda i, *_: (i, 0, 0, 0)),
                pl.BlockSpec((bv, t), lambda i, *_: (i, 0)),
                pl.BlockSpec((blocks, bn, t), lambda i, *_: (0, 0, 0)),
            ],
            out_specs=(
                pl.BlockSpec((1, touches, bv, bn), lambda i, *_: (i, 0, 0, 0)),
                pl.BlockSpec((1, touches, bn), lambda i, *_: (i, 0, 0)),
            ),
        ),
        name="foot_terms",
    )(my_block, footprints, data, full)


def spread_kernel(parts, grad, power, tiles, live, new, pair, cross, out, pgot, psem, csem, wsem):
    vblocks, touches, bv, bn = grad.shape
    rows = bv // parts
    me = lax.axis_index("frm")
    line, core = me // 2, lax.rem(me, 2)
    mate = line * 2 + 1 - core
    far = (1 - line) * 2 + core
    others = [lax.rem(me + k, parts) for k in range(1, parts)]
    greet([{"frm": peer} for peer in others])

    def remote(src, dst, send, recv, peer):
        return pltpu.make_async_remote_copy(
            src_ref=src,
            dst_ref=dst,
            send_sem=send,
            recv_sem=recv,
            device_id={"frm": peer},
            device_id_type=pl.DeviceIdType.MESH,
        )

    def quarter(index):
        return pl.ds(index * rows, rows)

    def to_mate(v, slot):
        target = (line if slot == 1 else 1 - line) * 2 + 1 - core
        return remote(
            grad.at[v, :, quarter(target)],
            pair.at[slot, v],
            psem.at[0, slot, v],
            psem.at[1, slot, v],
            mate,
        )

    def to_far(v):
        return remote(out.at[v], cross.at[v], csem.at[0, v], csem.at[1, v], far)

    def to_other(k):
        return remote(power, pgot.at[k - 1], wsem.at[0, k - 1], wsem.at[1, k - 1], others[k - 1])

    for v in range(vblocks):
        to_mate(v, 0).start()
    for k in range(1, parts):
        to_other(k).start()
    for v in range(vblocks):
        to_mate(v, 1).start()
    for v in range(vblocks):
        to_mate(v, 0).wait_recv()
        summed = grad[v, :, quarter(far)].astype(jnp.float32) + pair[0, v].astype(jnp.float32)
        out[v] = summed.astype(jnp.bfloat16)
        to_far(v).start()
    total = power[...]
    for k in range(1, parts):
        to_other(k).wait_recv()
        total = total + pgot[k - 1]
    scale = 1.0 / jnp.maximum(total, 1.0)
    for v in range(vblocks):
        to_mate(v, 1).wait_recv()
        to_far(v).wait_recv()
        for k in range(touches):
            moved = grad[v, k, quarter(me)].astype(jnp.float32) + pair[1, v, k].astype(jnp.float32)
            moved = moved + cross[v, k].astype(jnp.float32)
            old = tiles[v, k].astype(jnp.float32)
            moved = jnp.maximum(old + moved * scale[v, k : k + 1], 0.0)
            keep = (old > 0) & (live[v, k : k + 1] > 0)
            new[v, k] = jnp.where(keep, moved, 0.0).astype(jnp.bfloat16)
    for v in range(vblocks):
        to_mate(v, 0).wait_send()
        to_mate(v, 1).wait_send()
        to_far(v).wait_send()
    for k in range(1, parts):
        to_other(k).wait_send()


def spread_footprints(grad, power, tiles, live, parts):
    vblocks, touches, bv, bn = grad.shape
    shape = (vblocks, touches, bv // parts, bn)
    return pl.pallas_call(
        functools.partial(spread_kernel, parts),
        out_shape=jax.ShapeDtypeStruct(shape, jnp.bfloat16),
        in_specs=[pl.BlockSpec(memory_space=VMEM)] * 4,
        out_specs=pl.BlockSpec(memory_space=VMEM),
        scratch_shapes=[
            pltpu.VMEM((2,) + shape, jnp.bfloat16),
            pltpu.VMEM(shape, jnp.bfloat16),
            pltpu.VMEM(shape, jnp.bfloat16),
            pltpu.VMEM((parts - 1,) + power.shape, jnp.float32),
            pltpu.SemaphoreType.DMA((2, 2, vblocks)),
            pltpu.SemaphoreType.DMA((2, vblocks)),
            pltpu.SemaphoreType.DMA((2, parts - 1)),
        ],
        compiler_params=pltpu.CompilerParams(collective_id=2, has_side_effects=True),
        name="spread_footprints",
    )(grad, power, tiles, live)


def ring_body(data, footprints, traces, incidence, counts):
    n = lax.axis_size("vox")
    here = lax.axis_index("vox")
    parts = lax.axis_size("frm")
    vblocks, touches, bv, bn = footprints.shape
    nb = traces.shape[0]
    subs = 4 if nb % 4 == 0 else 2
    my_block = lax.dynamic_slice_in_dim(incidence, here * vblocks, vblocks)
    neuron = jnp.arange(bn, dtype=jnp.int32)
    own_counts = lax.dynamic_slice_in_dim(counts, here * nb, nb)
    live_own = (neuron[None, :] < own_counts[:, None]).astype(jnp.float32)
    entry_live = (neuron < counts[my_block][:, :, None]).astype(jnp.float32)
    rows = bv // parts
    tiles = lax.dynamic_slice_in_dim(footprints, lax.axis_index("frm") * rows, rows, 2)
    full = gather_traces(traces, n, subs)
    part, denom = terms(my_block, counts, footprints, data, full)
    new_traces, new_full = update_traces(part, denom, traces, live_own, n, subs)
    grad, power = foot_terms(my_block, footprints, data, new_full)
    new_footprints = spread_footprints(grad, power, tiles, entry_live, parts)
    return (new_traces, new_footprints)


highest = lax.Precision.HIGHEST


def entry_layout(incidence, owned_blocks, devices):
    per_device = incidence.reshape(devices, -1)
    owners = per_device // owned_blocks
    within = per_device - owners * owned_blocks
    entries = per_device.shape[1]
    position = jnp.arange(entries, dtype=jnp.int32)
    before = position[None, :] < position[:, None]
    same_owner = owners[:, :, None] == owners[:, None, :]
    ranks = jnp.sum((same_owner & before[None, :, :]).astype(jnp.int32), axis=2)
    return (per_device, owners, within, ranks)


def slot_body(data, footprints, traces, incidence, counts):
    devices = lax.axis_size("vox")
    here_index = lax.axis_index("vox")
    frame_parts = lax.axis_size("frm")
    frame_index = lax.axis_index("frm")
    vblocks, touches, block_vox, block_neurons = footprints.shape
    nblocks = traces.shape[0]
    frames = traces.shape[2]
    entries = vblocks * touches
    capacity = 2 * entries // devices
    slot_total = devices * capacity
    rows_quarter = block_vox // frame_parts
    per_device, owners, within, ranks = entry_layout(incidence, nblocks, devices)
    my_block = per_device[here_index]
    my_slot = owners[here_index] * capacity + ranks[here_index]
    from_here = owners == here_index
    sources = jnp.arange(devices, dtype=jnp.int32)[:, None]
    target = jnp.where(from_here, sources * capacity + ranks, slot_total).reshape(-1)
    slot_block = (
        jnp.full((slot_total,), nblocks, jnp.int32).at[target].set(within.reshape(-1), mode="drop")
    )
    neuron = jnp.arange(block_neurons, dtype=jnp.int32)
    own_counts = lax.dynamic_slice_in_dim(counts, here_index * nblocks, nblocks)
    live_own = neuron[None, :] < own_counts[:, None]
    table = jnp.arange(counts.shape[0], dtype=jnp.int32)
    entry_counts = jnp.sum(
        jnp.where(my_block[:, None] == table[None, :], counts[None, :], 0), axis=1
    )
    entry_live = neuron[None, :] < entry_counts[:, None]
    data_blocks = data.reshape(vblocks, block_vox, frames)

    def deliver(own_traces):
        piece = lax.all_gather(own_traces, "vox", axis=0, tiled=True)
        blocks_here = jnp.arange(piece.shape[0], dtype=jnp.int32)
        select = (my_block[:, None] == blocks_here[None, :]).astype(jnp.bfloat16)
        gathered = jnp.einsum("eb,bnf->enf", select, piece, preferred_element_type=jnp.float32)
        return gathered.astype(jnp.bfloat16)

    def residual(entry_traces):
        shaped = entry_traces.reshape(vblocks, touches, block_neurons, frames)
        recon = jnp.einsum("vkxn,vknf->vxf", footprints, shaped, preferred_element_type=jnp.float32)
        return (data_blocks.astype(jnp.float32) - recon).astype(jnp.bfloat16)

    alive = jnp.where(live_own[:, :, None], traces, jnp.zeros((), jnp.bfloat16))
    old_entries = deliver(alive)
    resid = residual(old_entries)
    term = jnp.einsum(
        "vkxn,vxf->vknf", footprints, resid, preferred_element_type=jnp.float32
    ).reshape(entries, block_neurons, frames)
    rowsum = jnp.sum(footprints, axis=(1, 3), dtype=jnp.float32)
    dterm = jnp.einsum(
        "vkxn,vx->vkn", footprints.astype(jnp.float32), rowsum, precision=highest
    ).reshape(entries, block_neurons)
    out_grad = jnp.zeros((slot_total, block_neurons, frames), jnp.float32).at[my_slot].set(term)
    out_denom = jnp.zeros((slot_total, block_neurons), jnp.float32).at[my_slot].set(dterm)
    got_grad, got_denom = (
        lax.all_to_all(out_grad, "vox", split_axis=0, concat_axis=0, tiled=True),
        lax.all_to_all(out_denom, "vox", split_axis=0, concat_axis=0, tiled=True),
    )
    grad = jax.ops.segment_sum(got_grad, slot_block, num_segments=nblocks + 1)[:nblocks]
    denom = jax.ops.segment_sum(got_denom, slot_block, num_segments=nblocks + 1)[:nblocks]
    updated = jnp.maximum(traces.astype(jnp.float32) + grad / denom[:, :, None], 0.0)
    new_traces = jnp.where(live_own[:, :, None], updated, 0.0).astype(jnp.bfloat16)
    new_entries = deliver(new_traces)
    resid_next = residual(new_entries)
    shaped_new = new_entries.reshape(vblocks, touches, block_neurons, frames)
    product = jnp.einsum(
        "vxf,vknf->xvkn", resid_next, shaped_new, preferred_element_type=jnp.float32
    )
    summed = lax.psum_scatter(
        product.reshape(rows_quarter * lax.axis_size("frm"), entries * block_neurons),
        "frm",
        scatter_dimension=0,
        tiled=True,
    )
    fgrad = summed.reshape(rows_quarter, vblocks, touches, block_neurons).transpose(1, 2, 0, 3)
    squares = jnp.sum(jnp.square(new_entries.astype(jnp.float32)), axis=2)
    power = lax.psum(squares, "frm")
    tiles = lax.dynamic_slice_in_dim(footprints, frame_index * rows_quarter, rows_quarter, 2)
    scale = jnp.maximum(power, 1.0).reshape(vblocks, touches, 1, block_neurons)
    keep = entry_live.reshape(vblocks, touches, 1, block_neurons) & (tiles > 0)
    moved = jnp.maximum(tiles.astype(jnp.float32) + fgrad / scale, 0.0)
    new_footprints = jnp.where(keep, moved, 0.0).astype(jnp.bfloat16)
    return (new_traces, new_footprints)


def body(data, footprints, traces, incidence, counts):
    devices = lax.axis_size("vox")
    entries = footprints.shape[0] * footprints.shape[1]
    dense = 2 * entries // devices >= traces.shape[0] and lax.axis_size("frm") == 4
    chosen = ring_body if dense else slot_body
    return chosen(data, footprints, traces, incidence, counts)


def solution(mesh):
    placed = (P("vox", "frm"), P("vox", None, None, None), P("vox", None, "frm"), P(), P())
    return jax.shard_map(
        body,
        mesh=mesh,
        in_specs=placed,
        out_specs=(P("vox", None, "frm"), P("vox", None, "frm", None)),
        check_vma=False,
    )
```
